256 devices in a mesh: dp: 64 (over z, x, core), tensor: 4 (over y).
Axes of the slice: x: 4, y: 4, z: 8, core: 2. Of those that a mesh axis runs over, the one named last changes fastest.
Arguments:
- gradients: float32 [64, 128, 3, 28672], P('dp', None, None, 'tensor'), may hold values from -2097152 to 2097152
- token_counts: int32 [64, 3], P('dp'), may hold values from 512 to 6143
- modality: int32 [64], P('dp'), may hold values from 0 to 2
- loss_weight: float32 [3], replicated, may hold values from 0.5 to 2
- master: float32 [128, 3, 28672], P('dp', None, 'tensor'), may hold values from -6 to 6
- moment_one: float32 [128, 3, 28672], P('dp', None, 'tensor'), may hold values from -6 to 6
- moment_two: float32 [128, 3, 28672], P('dp', None, 'tensor'), may hold values from 0.05 to 2
Outputs:
- new_master: float32 [128, 3, 28672], P('dp', None, 'tensor')
- new_moment_one: float32 [128, 3, 28672], P('dp', None, 'tensor')
- new_moment_two: float32 [128, 3, 28672], P('dp', None, 'tensor')
- working_weights: bfloat16 [128, 3, 28672], P(None, None, 'tensor')
The draws below stay inside these ranges and needn't reach their ends.
Inputs may be any that keep to these rules, and one draw needn't show every extreme that they name: `modality`: 0 is text, 1 image, 2 audio.
All inputs are finite; a program needn't handle non-finite values.
Results may differ from the reference program's by a relative error of at most 0.001.
Values may be sent and summed in bfloat16 or wider, within the bound.
No kernel may reach another device: no remote copies, remote signals or barrier semaphores. Data moves between devices by JAX's collectives and lax.ppermute only.
A program may use at most 128 MiB of HBM per device.

```python
import math
import jax
import jax.numpy as jnp
from jax import lax

FF = 28672
ROWS_DEV = 2
ROWS = 128
N_DP = 64


def draw_token_counts(key, part):
    replicas = ROWS // ROWS_DEV
    ranks = jnp.arange(replicas, dtype=jnp.int32)
    lowest = 512 + 1024 * ranks // max(replicas - 1, 1)
    counts = jax.random.randint(key, (replicas, 3), lowest[:, None], 4 * lowest[:, None], dtype=jnp.int32)
    counts = counts.at[0, 0].set(512)
    counts = counts.at[replicas - 1, 1].set(6143)
    return counts


def plant(entries, rng, low, top_value):
    longest = entries.shape.index(max(entries.shape))
    spots = []
    for shift in (0, 1):
        where = [jax.random.randint(jax.random.fold_in(rng, axis), (), 0, length) for axis, length in enumerate(entries.shape)]
        where[longest] = (where[longest] + shift) % entries.shape[longest]
        spots.append(tuple(where))
    return entries.at[spots[0]].set(low).at[spots[1]].set(top_value)


def raised(drawn, key, source, target, blocks, factor):
    owner, partner = [(jnp.arange(drawn.shape[dim]) // (drawn.shape[dim] // blocks)).reshape([-1 if axis == dim else 1 for axis in range(drawn.ndim)]) for dim in (source, target)]
    chosen = jax.random.permutation(key, blocks)[partner]
    strong = (owner == chosen) | (owner == (partner + blocks // 2) % blocks)
    return jnp.where(strong, factor * drawn, drawn)


def levels(rng, shape, shards, least, high):
    def one(axis_at, shards_of):
        draws = jax.random.uniform(jax.random.fold_in(jax.random.fold_in(rng, 6), axis_at), (shards_of,), jnp.float32, least / len(shards), high / len(shards))
        return jnp.repeat(jnp.exp(draws), shape[axis_at] // shards_of).reshape((-1,) + (1,) * (len(shape) - axis_at - 1))

    loudness = one(*shards[0])
    for cut in shards[1:]:
        loudness = loudness * one(*cut)
    return loudness


def centred(key, extent, width, reach, cuts=(), kind=jnp.bfloat16):
    level = levels(key, extent, cuts, -0.22, 0.18) if cuts else 1.0
    values = jax.random.normal(key, extent, jnp.float32) * width * level
    return jnp.minimum(jnp.maximum(values, -reach), reach).astype(kind)


def gaussian_with(own_key, dims, scale, most, pieces, heavy, held_as=jnp.bfloat16):
    values = scale * jax.random.normal(own_key, dims, jnp.float32)
    if pieces:
        values = values * levels(own_key, dims, pieces, -0.22, 0.18)
    return jnp.clip(raised(values, jax.random.fold_in(own_key, 3), *heavy), -most, most).astype(held_as)


def setup_inputs(seed: int = 0) -> dict:
    key_of = jax.random.split(jax.random.key(seed), 8)
    gradients = gaussian_with(key_of[0], (N_DP, ROWS, 3, FF), (1920 * N_DP), 2097152, ((0, 64), (3, 4)), (0, 1, 64, 4.0), jnp.float32)
    token_counts = draw_token_counts(jax.random.fold_in(key_of[7], 71), 0)
    modality = plant(jax.random.randint(key_of[2], (N_DP,), 0, 3), jax.random.fold_in(key_of[2], 1), 0, 2).astype(jnp.int32)
    loss_weight = jnp.clip(jnp.exp(jax.random.uniform(key_of[3], (3,), jnp.float32, math.log(0.5), math.log(2.0))), 0.5, 2.0)
    master = centred(key_of[4], (ROWS, 3, FF), 1.0, 6.0, ((0, 64), (2, 4)), jnp.float32)
    moment_one = centred(key_of[5], (ROWS, 3, FF), 0.5, 6.0, ((0, 64), (2, 4)), jnp.float32)
    moment_two = jnp.clip(jnp.exp(math.log(2.0) - 3.6888794 * jax.random.uniform(key_of[6], (ROWS, 3, FF), jnp.float32) ** levels(key_of[6], (ROWS, 3, FF), ((0, 64), (2, 4)), -0.2, 0.2)), 0.05, 2.0)
    return dict(gradients=gradients, token_counts=token_counts, modality=modality, loss_weight=loss_weight, master=master, moment_one=moment_one, moment_two=moment_two)


beta_one = 0.9
beta_two = 0.95
bias_one = 1.0 - 0.9 ** 10
bias_two = 1.0 - 0.95 ** 10
epsilon = 1e-08
learn_rate = 0.01
decay_rate = 0.1

def adam_update(grad_sum, first, second, weights):
    first_new = beta_one * first + (1.0 - beta_one) * grad_sum
    second_new = beta_two * second + (1.0 - beta_two) * grad_sum * grad_sum
    step_size = first_new / bias_one / (jnp.sqrt(second_new / bias_two) + epsilon)
    weights_new = weights - learn_rate * (step_size + decay_rate * weights)
    return (weights_new, first_new, second_new)

def reference(gradients, token_counts, modality, loss_weight, master, moment_one, moment_two):
    totals = lax.optimization_barrier(jnp.sum(token_counts, axis=0)).astype(jnp.float32)
    ratios = loss_weight / totals
    picked = (modality[:, None] == jnp.arange(3, dtype=jnp.int32)[None, :]).astype(jnp.float32)
    scales = lax.optimization_barrier(jnp.sum(picked * ratios[None, :], axis=1))

    def accumulate(running, paired):
        return (running + paired[0] * paired[1], None)
    grad_sum, ignored = lax.scan(accumulate, jnp.zeros(gradients.shape[1:], jnp.float32), (gradients, scales))
    weights_new, first_new, second_new = adam_update(grad_sum, moment_one, moment_two, master)
    return (weights_new, first_new, second_new, weights_new.astype(jnp.bfloat16))
```

```python
import jax
import jax.numpy as jnp
from jax import lax
from jax.sharding import Mesh
from jax.sharding import PartitionSpec as P

DP = ("z", "x", "c")

beta_one = 0.9
beta_two = 0.95
bias_one = 1.0 - 0.9**10
bias_two = 1.0 - 0.95**10
epsilon = 1e-08
learn_rate = 0.01
decay_rate = 0.1

PART_A = 1536
RAISE = 4.0
LINK = jnp.float16


def adam_update(grad_sum, first, second, weights):
    first_new = beta_one * first + (1.0 - beta_one) * grad_sum
    second_new = beta_two * second + (1.0 - beta_two) * grad_sum * grad_sum
    step_size = first_new / bias_one / (jnp.sqrt(second_new / bias_two) + epsilon)
    weights_new = weights - learn_rate * (step_size + decay_rate * weights)
    return (weights_new, first_new, second_new)


def shift(value, axis, by):
    n = lax.axis_size(axis)
    return lax.ppermute(value, axis, [(i, (i + by) % n) for i in range(n)])


def trade(value, axis, bit):
    n = lax.axis_size(axis)
    return lax.ppermute(value, axis, [(i, i ^ bit) for i in range(n)])


def sum_exchange(part, axis):
    n = lax.axis_size(axis)
    arrived = [shift(part(k).astype(LINK), axis, k) for k in range(1, n)]
    total = part(0)
    for piece in arrived:
        total = total + piece.astype(jnp.float32)
    return total


def gather_exchange(own, axis, dim):
    n, me, width = lax.axis_size(axis), lax.axis_index(axis), own.shape[dim]
    arrived = [own] + [shift(own, axis, k) for k in range(1, n)]
    shape = list(own.shape)
    shape[dim] = n * width
    whole = jnp.zeros(shape, own.dtype)
    for k, piece in enumerate(arrived):
        whole = lax.dynamic_update_slice_in_dim(whole, piece, width * lax.rem(me - k + n, n), dim)
    return whole


def totals_of(counts):
    for axis, bit in (("c", 1), ("x", 1), ("x", 2), ("z", 1), ("z", 2), ("z", 4)):
        if bit < lax.axis_size(axis):
            counts = counts + trade(counts, axis, bit)
    return counts


def split_columns(state, half, part_a, part_b):
    me, mine = lax.axis_index("x"), lax.axis_index("c")
    keep = lax.dynamic_slice_in_dim(state, mine * half, half, 3)
    give = lax.dynamic_slice_in_dim(state, (1 - mine) * half, half, 3)
    got = trade(give, "c", 1)
    first = jnp.where(mine == 0, keep, got)
    second = jnp.where(mine == 0, got, keep)
    rows = jnp.concatenate([first, second], axis=2)

    def piece(k):
        at = lax.rem(me + k, 4)
        return jnp.concatenate(
            [
                lax.dynamic_slice_in_dim(rows, part_a * at, part_a, 3),
                lax.dynamic_slice_in_dim(rows, 4 * part_a + part_b * at, part_b, 3),
            ],
            axis=3,
        )

    pieces = [piece(0)] + [shift(piece(k), "x", k) for k in range(1, 4)]
    whole = jnp.zeros((*state.shape[:2], 16, part_a + part_b), state.dtype)
    for k, got in enumerate(pieces):
        whole = lax.dynamic_update_slice_in_dim(whole, got, 4 * lax.rem(me - k + 4, 4), 2)
    return whole


def join_columns(state, half, part_a, part_b):
    me, mine = lax.axis_index("x"), lax.axis_index("c")

    def piece(k):
        return lax.dynamic_slice_in_dim(state, 4 * lax.rem(me + k, 4), 4, 2)

    pieces = [piece(0)] + [shift(piece(k), "x", k) for k in range(1, 4)]
    left = jnp.zeros((*state.shape[:2], 4, half), state.dtype)
    for k, got in enumerate(pieces):
        at = lax.rem(me - k + 4, 4)
        left = lax.dynamic_update_slice_in_dim(left, got[..., :part_a], part_a * at, 3)
        left = lax.dynamic_update_slice_in_dim(left, got[..., part_a:], 4 * part_a + part_b * at, 3)
    keep = lax.dynamic_slice_in_dim(left, 2 * mine, 2, 2)
    give = lax.dynamic_slice_in_dim(left, 2 * (1 - mine), 2, 2)
    got = trade(give, "c", 1)
    first = jnp.where(mine == 0, keep, got)
    second = jnp.where(mine == 0, got, keep)
    return jnp.concatenate([first, second], axis=3)


def local(gradients, token_counts, modality, loss_weight, master, moment_one, moment_two):
    grad = jnp.transpose(gradients[0], (1, 0, 2))
    mats, rows, cols = grad.shape
    half = cols // 2
    wide_a, wide_b = PART_A, half - PART_A
    part_a, part_b = wide_a // 4, wide_b // 4
    depth, across, mine = lax.axis_index("z"), lax.axis_index("x"), lax.axis_index("c")
    block = rows // 8

    there = (1 - mine) * half
    raw_a = trade(lax.dynamic_slice_in_dim(grad, there, wide_a, 2), "c", 1)
    raw_b = trade(lax.dynamic_slice_in_dim(grad, there + wide_a, wide_b, 2), "c", 1)

    totals = totals_of(token_counts[0]).astype(jnp.float32)
    ratios = loss_weight / totals
    kinds = jnp.concatenate([modality, trade(modality, "c", 1)])
    picked = (lax.iota(jnp.int32, 3)[None, :] == kinds[:, None]).astype(jnp.float32)
    scales = jnp.sum(picked * ratios[None, :], axis=1) * RAISE

    here = mine * half

    def for_z(k):
        at = block * lax.rem(depth + k, 8)
        own = lax.dynamic_slice(grad, (0, at, here), (mats, block, wide_a))
        other = lax.dynamic_slice(raw_a, (0, at, 0), (mats, block, wide_a))
        return own * scales[0] + other * scales[1]

    def for_x(k):
        at = part_b * lax.rem(across + k, 4)
        own = lax.dynamic_slice(grad, (0, 0, here + wide_a + at), (mats, rows, part_b))
        other = lax.dynamic_slice(raw_b, (0, 0, at), (mats, rows, part_b))
        return own * scales[0] + other * scales[1]

    sum_a = sum_exchange(for_z, "z")
    sum_b = sum_exchange(for_x, "x")
    sum_a = sum_exchange(
        lambda k: lax.dynamic_slice_in_dim(sum_a, part_a * lax.rem(across + k, 4), part_a, 2), "x"
    )
    sum_b = sum_exchange(
        lambda k: lax.dynamic_slice_in_dim(sum_b, block * lax.rem(depth + k, 8), block, 1), "z"
    )
    summed = jnp.concatenate([sum_a, sum_b], axis=2) * (1.0 / RAISE)

    state = jnp.stack([jnp.transpose(a, (1, 0, 2)) for a in (master, moment_one, moment_two)])
    state = split_columns(state, half, part_a, part_b)
    new = adam_update(summed, state[1], state[2], state[0])
    lean = new[0].astype(jnp.bfloat16)

    lean_a = gather_exchange(lean[..., :part_a], "x", 2)
    lean_b = gather_exchange(lean[..., part_a:], "z", 1)
    lean_a = gather_exchange(lean_a, "z", 1)
    lean_b = gather_exchange(lean_b, "x", 2)
    far_a, far_b = trade(lean_a, "c", 1), trade(lean_b, "c", 1)
    whole = jnp.zeros((mats, rows, cols), jnp.bfloat16)
    for at, piece in ((here, lean_a), (here + wide_a, lean_b), (there, far_a), (there + wide_a, far_b)):
        whole = lax.dynamic_update_slice_in_dim(whole, piece, at, 2)

    back = join_columns(jnp.stack(new), half, part_a, part_b)
    outs = [jnp.transpose(back[i], (1, 0, 2)) for i in range(3)]
    return (*outs, jnp.transpose(whole, (1, 0, 2)))


def solution(mesh):
    torus = Mesh(mesh.devices.reshape(8, 4, 2, mesh.shape["tensor"]), (*DP, "tensor"))
    in_specs = (
        P(DP, None, None, "tensor"),
        P(DP, None),
        P(DP),
        P(),
        P(DP, None, "tensor"),
        P(DP, None, "tensor"),
        P(DP, None, "tensor"),
    )
    out_specs = (
        P(DP, None, "tensor"),
        P(DP, None, "tensor"),
        P(DP, None, "tensor"),
        P(None, None, "tensor"),
    )
    return jax.shard_map(local, mesh=torus, in_specs=in_specs, out_specs=out_specs, check_vma=False)
```

```python
import jax
import jax.numpy as jnp
from jax import lax
from jax.sharding import Mesh
from jax.sharding import PartitionSpec as P

DP = ("z", "x", "c")
DEEP, WIDE = 8, 4

beta_one = 0.9
beta_two = 0.95
bias_one = 1.0 - 0.9**10
bias_two = 1.0 - 0.95**10
epsilon = 1e-08
learn_rate = 0.01
decay_rate = 0.1

PART_A = 1536
RAISE = 4.0
LINK = jnp.float16


def adam_update(grad_sum, first, second, weights):
    first_new = beta_one * first + (1.0 - beta_one) * grad_sum
    second_new = beta_two * second + (1.0 - beta_two) * grad_sum * grad_sum
    step_size = first_new / bias_one / (jnp.sqrt(second_new / bias_two) + epsilon)
    weights_new = weights - learn_rate * (step_size + decay_rate * weights)
    return (weights_new, first_new, second_new)


def x_partner(step, z, x, c):
    return (z, x ^ (1 if step == c else 3), c)


def z_partner(step, z, x, c):
    if step == 2:
        return (z ^ 4, x, c)
    return ((((z + c) % DEEP) ^ (1 << step)) - c) % DEEP, x, c


def core_partner(step, z, x, c):
    return (z, x, 1 - c)


def trade(value, partner, step=0):
    def index(z, x, c):
        return (z * WIDE + x) * 2 + c

    perm = [
        (index(z, x, c), index(*partner(step, z, x, c)))
        for z in range(DEEP)
        for x in range(WIDE)
        for c in range(2)
    ]
    return lax.ppermute(value, DP, perm)


def x_bits(x, c):
    high, mixed = x // 2, (x + x // 2) % 2
    return (mixed * (1 - c) + high * c, high * (1 - c) + mixed * c)


def pick(value, index, parts, dim):
    size = value.shape[dim] // parts
    return lax.dynamic_slice_in_dim(value, index * size, size, dim)


def sum_x(value, bits):
    for step in range(2):
        got = trade(pick(value, 1 - bits[step], 2, 2).astype(LINK), x_partner, step)
        value = pick(value, bits[step], 2, 2) + got.astype(jnp.float32)
    return value


def pick_rows(value, index):
    mats, rows, cols = value.shape
    split = value.reshape(mats, rows // 32, 2, 16, cols)
    return lax.dynamic_slice_in_dim(split, index, 1, 2).reshape(mats, rows // 2, cols)


def sum_z(value, depth):
    for step in range(3):
        bit = (depth // 2**step) % 2
        got = trade(pick_rows(value, 1 - bit).astype(LINK), z_partner, step)
        value = pick_rows(value, bit) + got.astype(jnp.float32)
    return value


def both(own, got, bit, dim):
    first = jnp.where(bit == 0, own, got)
    second = jnp.where(bit == 0, got, own)
    return jnp.concatenate([first, second], axis=dim)


def gather_x(value, bits):
    for step in (1, 0):
        value = both(value, trade(value, x_partner, step), bits[step], 2)
    return value


def gather_z(value, depth):
    mats, _, cols = value.shape
    for step in (2, 1, 0):
        got = trade(value, z_partner, step)
        bit = (depth // 2**step) % 2
        rows = value.shape[1]
        own, got = (v.reshape(mats, rows // 16, 1, 16, cols) for v in (value, got))
        value = both(own, got, bit, 2).reshape(mats, 2 * rows, cols)
    return value


def split_columns(state, wide_a, across, mine, bits):
    keep = pick(state, mine, 2, 3)
    got = trade(pick(state, 1 - mine, 2, 3), core_partner)
    rows = both(keep, got, mine, 2)
    groups = [(rows[..., :wide_a], rows[..., wide_a:])]
    for step in range(2):
        give = [[pick(v, 1 - bits[step], 2, 3) for v in group] for group in groups]
        flat = jnp.concatenate([jnp.concatenate(g, axis=3) for g in give], axis=2)
        got = trade(flat, x_partner, step)
        cut = give[0][0].shape[3]
        groups = [tuple(pick(v, bits[step], 2, 3) for v in group) for group in groups]
        for k in range(len(give)):
            piece = got[:, :, 4 * k : 4 * k + 4]
            groups.append((piece[..., :cut], piece[..., cut:]))
    masks = (1 + 2 * mine, 3 - 2 * mine)
    places = (across, across ^ masks[0], across ^ masks[1], across ^ masks[0] ^ masks[1])
    whole = jnp.zeros((*state.shape[:2], 16, state.shape[3] // 8), state.dtype)
    for place, group in zip(places, groups):
        whole = lax.dynamic_update_slice_in_dim(whole, jnp.concatenate(group, axis=3), 4 * place, 2)
    return whole


def join_columns(state, wide_a, across, mine, bits):
    masks = (1 + 2 * mine, 3 - 2 * mine)
    places = (across, across ^ masks[0], across ^ masks[1], across ^ masks[0] ^ masks[1])
    own, one, two, three = [pick(state, place, 4, 2) for place in places]
    got = trade(jnp.concatenate([one, three], axis=2), x_partner, 0)
    mine_now = [own, got[:, :, :4]]
    got = trade(jnp.concatenate([two, got[:, :, 4:]], axis=2), x_partner, 1)
    chunks = [*mine_now, got[:, :, :4], got[:, :, 4:]]
    place = 2 * bits[0] + bits[1]
    cut, rest = wide_a // 4, state.shape[3] - wide_a // 4
    left = jnp.zeros((*state.shape[:2], 4, 4 * state.shape[3]), state.dtype)
    for chunk, flip in zip(chunks, (0, 2, 1, 3)):
        at = place ^ flip
        left = lax.dynamic_update_slice_in_dim(left, chunk[..., :cut], cut * at, 3)
        left = lax.dynamic_update_slice_in_dim(left, chunk[..., cut:], wide_a + rest * at, 3)
    keep = pick(left, mine, 2, 2)
    got = trade(pick(left, 1 - mine, 2, 2), core_partner)
    return both(keep, got, mine, 3)


def local(gradients, token_counts, modality, loss_weight, master, moment_one, moment_two):
    grad = jnp.transpose(gradients[0], (1, 0, 2))
    mats, rows, cols = grad.shape
    half = cols // 2
    wide_a, wide_b = PART_A, half - PART_A
    depth, across, mine = (lax.axis_index(a) for a in DP)
    bits = x_bits(across, mine)

    counts = jnp.broadcast_to(token_counts, (DEEP * WIDE * 2, 3))[:, None]
    totals = lax.all_to_all(counts, DP, 0, 0, tiled=True).sum(axis=(0, 1)).astype(jnp.float32)

    here, there = mine * half, (1 - mine) * half
    raw_a = trade(lax.dynamic_slice_in_dim(grad, there, wide_a, 2), core_partner)
    raw_b = trade(lax.dynamic_slice_in_dim(grad, there + wide_a, wide_b, 2), core_partner)

    ratios = loss_weight / totals
    kinds = jnp.concatenate([modality, trade(modality, core_partner)])
    picked = (lax.iota(jnp.int32, 3)[None, :] == kinds[:, None]).astype(jnp.float32)
    scales = jnp.sum(picked * ratios[None, :], axis=1) * RAISE

    own_a = lax.dynamic_slice_in_dim(grad, here, wide_a, 2)
    own_b = lax.dynamic_slice_in_dim(grad, here + wide_a, wide_b, 2)
    sum_a = sum_x(sum_z(own_a * scales[0] + raw_a * scales[1], depth), bits)
    sum_b = sum_z(sum_x(own_b * scales[0] + raw_b * scales[1], bits), depth)
    summed = jnp.concatenate([sum_a, sum_b], axis=2) * (1.0 / RAISE)

    state = jnp.stack([jnp.transpose(a, (1, 0, 2)) for a in (master, moment_one, moment_two)])
    state = split_columns(state, wide_a, across, mine, bits)
    new = adam_update(summed, state[1], state[2], state[0])
    lean = new[0].astype(jnp.bfloat16)

    lean_a = gather_z(gather_x(lean[..., : wide_a // 4], bits), depth)
    lean_b = gather_x(gather_z(lean[..., wide_a // 4 :], depth), bits)
    far_a, far_b = trade(lean_a, core_partner), trade(lean_b, core_partner)
    whole = jnp.zeros((mats, rows, cols), jnp.bfloat16)
    for at, piece in ((here, lean_a), (here + wide_a, lean_b), (there, far_a), (there + wide_a, far_b)):
        whole = lax.dynamic_update_slice_in_dim(whole, piece, at, 2)

    back = join_columns(jnp.stack(new), wide_a, across, mine, bits)
    outs = [jnp.transpose(back[i], (1, 0, 2)) for i in range(3)]
    return (*outs, jnp.transpose(whole, (1, 0, 2)))


def solution(mesh):
    torus = Mesh(mesh.devices.reshape(DEEP, WIDE, 2, mesh.shape["tensor"]), (*DP, "tensor"))
    in_specs = (
        P(DP, None, None, "tensor"),
        P(DP, None),
        P(DP),
        P(),
        P(DP, None, "tensor"),
        P(DP, None, "tensor"),
        P(DP, None, "tensor"),
    )
    out_specs = (
        P(DP, None, "tensor"),
        P(DP, None, "tensor"),
        P(DP, None, "tensor"),
        P(None, None, "tensor"),
    )
    return jax.shard_map(local, mesh=torus, in_specs=in_specs, out_specs=out_specs, check_vma=False)
```

```python
import jax
import jax.numpy as jnp
from jax import lax
from jax.experimental import pallas as pl
from jax.experimental.pallas import tpu as pltpu
from jax.sharding import Mesh
from jax.sharding import PartitionSpec as P

DP = ("z", "x", "c")
DEEP, WIDE = 8, 4

beta_one = 0.9
beta_two = 0.95
bias_one = 1.0 - 0.9**10
bias_two = 1.0 - 0.95**10
epsilon = 1e-08
learn_rate = 0.01
decay_rate = 0.1

RAISE = 4.0
LINK = jnp.float16


def adam_update(grad_sum, first, second, weights):
    first_new = beta_one * first + (1.0 - beta_one) * grad_sum
    second_new = beta_two * second + (1.0 - beta_two) * grad_sum * grad_sum
    step_size = first_new / bias_one / (jnp.sqrt(second_new / bias_two) + epsilon)
    weights_new = weights - learn_rate * (step_size + decay_rate * weights)
    return (weights_new, first_new, second_new)


def x_partner(step, z, x, c):
    return (z, x ^ (1 if step == c else 3), c)


def z_partner(step, z, x, c):
    return ((((z + c) % DEEP) ^ 1) - c) % DEEP, x, c


def z_ahead(step, z, x, c):
    return (z + 2 * step) % DEEP, x, c


def core_partner(step, z, x, c):
    return (z, x, 1 - c)


def trade(value, partner, step=0):
    def index(z, x, c):
        return (z * WIDE + x) * 2 + c

    perm = [
        (index(z, x, c), index(*partner(step, z, x, c)))
        for z in range(DEEP)
        for x in range(WIDE)
        for c in range(2)
    ]
    return lax.ppermute(value, DP, perm)


def x_bits(x, c):
    high, mixed = x // 2, (x + x // 2) % 2
    return (mixed * (1 - c) + high * c, high * (1 - c) + mixed * c)


def pick(value, index, parts, dim):
    size = value.shape[dim] // parts
    return lax.dynamic_slice_in_dim(value, index * size, size, dim)


def send(value, partner, step):
    return trade(value.astype(LINK), partner, step).astype(jnp.float32)


def both(own, got, bit, dim):
    first = jnp.where(bit == 0, own, got)
    second = jnp.where(bit == 0, got, own)
    return jnp.concatenate([first, second], axis=dim)


def pick_z(value, index):
    mats, blocks, *rest = value.shape
    pairs = value.reshape(mats, blocks // 2, 2, *rest)
    return lax.dynamic_slice_in_dim(pairs, index, 1, 2).reshape(mats, blocks // 2, *rest)


def sum_x(value, bits, step):
    got = send(pick(value, 1 - bits[step], 2, 3), x_partner, step)
    return pick(value, bits[step], 2, 3) + got


def sum_z(value, odd):
    got = send(pick_z(value, 1 - odd), z_partner, 0)
    return pick_z(value, odd) + got


FAR = (2, 1, 3)


def sum_quad(value, place):
    got = [send(pick(value, (place + k) % 4, 4, 1), z_ahead, k) for k in FAR]
    return pick(value, place, 4, 1) + got[0] + got[1] + got[2]


def gather_quad(value, place):
    mats, _, *rest = value.shape
    got = [trade(value, z_ahead, k) for k in FAR]
    whole = jnp.zeros((mats, 4, *rest), value.dtype)
    for k, piece in zip((0, *FAR), (value, *got)):
        whole = lax.dynamic_update_slice_in_dim(whole, piece, (place - k) % 4, 1)
    return whole


def gather_x(value, bits, step):
    return both(value, trade(value, x_partner, step), bits[step], 3)


def gather_z(value, odd):
    mats, blocks, *rest = value.shape
    got = trade(value, z_partner, 0)
    own, got = (v.reshape(mats, blocks, 1, *rest) for v in (value, got))
    return both(own, got, odd, 2).reshape(mats, 2 * blocks, *rest)


def x_places(across, mine):
    masks = (1 + 2 * mine, 3 - 2 * mine)
    return (across, across ^ masks[0], across ^ masks[1], across ^ masks[0] ^ masks[1])


def split_step(groups, bits, step):
    give = jnp.concatenate([pick(v, 1 - bits[step], 2, 3) for v in groups], axis=2)
    got = trade(give, x_partner, step)
    groups = [pick(v, bits[step], 2, 3) for v in groups]
    return groups + [got[:, :, 4 * k : 4 * k + 4] for k in range(len(groups))]


def rows_in_order(groups, across, mine):
    one = groups[0]
    whole = jnp.zeros((*one.shape[:2], 16, one.shape[3]), one.dtype)
    for place, group in zip(x_places(across, mine), groups):
        whole = lax.dynamic_update_slice_in_dim(whole, group, 4 * place, 2)
    return whole


def join_columns(state, across, mine, bits):
    own, one, two, three = [pick(state, place, 4, 2) for place in x_places(across, mine)]
    got = trade(jnp.concatenate([one, three], axis=2), x_partner, 0)
    first = got[:, :, :4]
    got = trade(jnp.concatenate([two, got[:, :, 4:]], axis=2), x_partner, 1)
    place, width = 2 * bits[0] + bits[1], state.shape[3]
    left = jnp.zeros((*state.shape[:2], 4, 4 * width), state.dtype)
    for chunk, flip in zip((own, first, got[:, :, :4], got[:, :, 4:]), (0, 2, 1, 3)):
        left = lax.dynamic_update_slice_in_dim(left, chunk, width * (place ^ flip), 3)
    return left


def scale_kernel(at_ref, notes_ref, weight_ref, own_ref, raw_ref):
    totals = jnp.sum(notes_ref[...], axis=0).astype(jnp.float32)
    ratios = weight_ref[...] / totals
    lanes = lax.broadcasted_iota(jnp.int32, ratios.shape, 1)
    for j, out in enumerate((own_ref, raw_ref)):
        kind = notes_ref[at_ref[j]][:, 3:4]
        picked = jnp.sum(jnp.where(lanes == kind, ratios, 0.0), axis=1, keepdims=True)
        out[...] = jnp.broadcast_to(picked * RAISE, out.shape)


def scale_rows(notes, loss_weight, places, width):
    weight = jnp.pad(loss_weight, (0, 1))[None]
    return pl.pallas_call(
        scale_kernel,
        out_shape=[jax.ShapeDtypeStruct((1, width), jnp.float32)] * 2,
        in_specs=[
            pl.BlockSpec(memory_space=pltpu.SMEM),
            pl.BlockSpec(memory_space=pltpu.VMEM),
            pl.BlockSpec(memory_space=pltpu.VMEM),
        ],
        out_specs=[pl.BlockSpec(memory_space=pltpu.VMEM)] * 2,
        compiler_params=pltpu.CompilerParams(vmem_limit_bytes=1 << 20),
    )(places, notes, weight)


def local(gradients, token_counts, modality, loss_weight, master, moment_one, moment_two):
    mats, rows, cols = 3, gradients.shape[1], gradients.shape[3]
    half = cols // 2
    depth, across, mine = (lax.axis_index(a) for a in DP)
    odd, place = depth % 2, depth // 2
    xb = x_bits(across, mine)

    notes = jnp.concatenate([token_counts, modality[:, None]], axis=1)
    notes = jnp.broadcast_to(notes, (DEEP * WIDE * 2, 4))[:, None]
    notes = lax.all_to_all(notes, DP, 0, 0, tiled=True)

    grad = jnp.transpose(gradients[0], (1, 0, 2)).reshape(mats, DEEP, 2, 8, cols)

    def tile(grad, t, core):
        cut = lax.dynamic_slice(grad, (0, 0, t, 0, core * half), (mats, DEEP, 1, 8, half))
        return cut.reshape(mats, DEEP, 8, half)

    give_a = tile(grad, 0, 1 - mine)
    grad, give_a = lax.optimization_barrier((grad, give_a))
    give_b = tile(grad, 1, 1 - mine)
    grad, give_b = lax.optimization_barrier((grad, give_b))
    own = [tile(grad, t, mine) for t in range(2)]
    raw_a = trade(give_a, core_partner)
    raw_b = trade(give_b, core_partner)
    raw = [raw_a, raw_b]

    state = jnp.stack([jnp.transpose(a, (1, 0, 2)) for a in (master, moment_one, moment_two)])
    got = trade(pick(state, 1 - mine, 2, 3), core_partner)
    state = both(pick(state, mine, 2, 3), got, mine, 2)

    chip = 2 * (WIDE * depth + across)
    scales = scale_rows(notes, loss_weight, jnp.stack([chip + mine, chip + 1 - mine]), half)

    def combined(t, cut):
        wide = cut(own[t])
        first, second = (scale[:, : wide.shape[3]] for scale in scales)
        return wide * first + cut(raw[t]) * second

    give_a = combined(0, lambda v: pick_z(v, 1 - odd)).astype(LINK)
    give_b = combined(1, lambda v: pick(v, 1 - xb[0], 2, 3)).astype(LINK)
    raw_a, give_a = lax.optimization_barrier((raw[0], give_a))
    raw_b, give_b = lax.optimization_barrier((raw[1], give_b))
    raw = [raw_a, raw_b]
    part_a = lax.optimization_barrier(combined(0, lambda v: pick_z(v, odd)))
    part_b = lax.optimization_barrier(combined(1, lambda v: pick(v, xb[0], 2, 3)))
    got_a = send(give_a, z_partner, 0)
    got_b = send(give_b, x_partner, 0)
    part_a, part_b = part_a + got_a, part_b + got_b
    part_a = sum_x(part_a, xb, 0)
    part_b = sum_z(part_b, odd)
    groups = split_step([state], xb, 0)
    part = jnp.concatenate([part_a, part_b], axis=2)
    give_c = pick(part, 1 - xb[1], 2, 3).astype(LINK)
    got = trade(give_c, x_partner, 1)
    groups = split_step(groups, xb, 1)
    part = lax.optimization_barrier(pick(part, xb[1], 2, 3) + got.astype(jnp.float32))

    state = rows_in_order(groups, across, mine)

    summed = sum_quad(part, place)[:, 0] * (1.0 / RAISE)
    new = adam_update(summed, state[1], state[2], state[0])
    lean = new[0].astype(jnp.bfloat16)[:, None]

    lean = gather_quad(lean, place)
    lean = gather_x(lean, xb, 1)
    lean_a = gather_x(lean[:, :, :8], xb, 0)
    lean_b = gather_z(lean[:, :, 8:], odd)
    got_a, got_b = trade(lean_a, z_partner), trade(lean_b, x_partner, 0)
    whole = jnp.zeros((mats, DEEP // 2, 2, 2, 8, cols), jnp.bfloat16)
    for core in (mine, 1 - mine):
        side = x_bits(across, core)[0]
        for tile_a, tile_b, place_a, place_b in (
            (lean_a, lean_b, odd, side),
            (got_a, got_b, 1 - odd, 1 - side),
        ):
            if core is not mine:
                tile_a, tile_b = trade(tile_a, core_partner), trade(tile_b, core_partner)
            tile_a = tile_a[:, :, None, None]
            whole = lax.dynamic_update_slice(whole, tile_a, (0, 0, place_a, 0, 0, core * half))
            tile_b = tile_b.reshape(mats, DEEP // 2, 2, 1, 8, half // 2)
            at = core * half + place_b * (half // 2)
            whole = lax.dynamic_update_slice(whole, tile_b, (0, 0, 0, 1, 0, at))
    whole = whole.reshape(mats, rows, cols)

    left = join_columns(jnp.stack(new), across, mine, xb)
    back = both(pick(left, mine, 2, 2), trade(pick(left, 1 - mine, 2, 2), core_partner), mine, 3)
    outs = [jnp.transpose(back[i], (1, 0, 2)) for i in range(3)]
    return (*outs, jnp.transpose(whole, (1, 0, 2)))


def solution(mesh):
    torus = Mesh(mesh.devices.reshape(DEEP, WIDE, 2, mesh.shape["tensor"]), (*DP, "tensor"))
    in_specs = (
        P(DP, None, None, "tensor"),
        P(DP, None),
        P(DP),
        P(),
        P(DP, None, "tensor"),
        P(DP, None, "tensor"),
        P(DP, None, "tensor"),
    )
    out_specs = (
        P(DP, None, "tensor"),
        P(DP, None, "tensor"),
        P(DP, None, "tensor"),
        P(None, None, "tensor"),
    )

    return jax.shard_map(local, mesh=torus, in_specs=in_specs, out_specs=out_specs, check_vma=False)
```

```python
import jax
import jax.numpy as jnp
from jax import lax
from jax.experimental import pallas as pl
from jax.experimental.pallas import tpu as pltpu
from jax.sharding import Mesh
from jax.sharding import PartitionSpec as P

DP = ("z", "x", "c")
DEEP, WIDE = 8, 4

beta_one = 0.9
beta_two = 0.95
bias_one = 1.0 - 0.9**10
bias_two = 1.0 - 0.95**10
epsilon = 1e-08
learn_rate = 0.01
decay_rate = 0.1

RAISE = 4.0
LINK = jnp.float16


def adam_update(grad_sum, first, second, weights):
    first_new = beta_one * first + (1.0 - beta_one) * grad_sum
    second_new = beta_two * second + (1.0 - beta_two) * grad_sum * grad_sum
    step_size = first_new / bias_one / (jnp.sqrt(second_new / bias_two) + epsilon)
    weights_new = weights - learn_rate * (step_size + decay_rate * weights)
    return (weights_new, first_new, second_new)


def x_partner(step, z, x, c):
    return (z, x ^ (1 if step == c else 3), c)


def z_partner(step, z, x, c):
    return ((((z + c) % DEEP) ^ 1) - c) % DEEP, x, c


def z_ahead(step, z, x, c):
    return (z + 2 * step) % DEEP, x, c


def core_partner(step, z, x, c):
    return (z, x, 1 - c)


def trade(value, partner, step=0):
    def index(z, x, c):
        return (z * WIDE + x) * 2 + c

    perm = [
        (index(z, x, c), index(*partner(step, z, x, c)))
        for z in range(DEEP)
        for x in range(WIDE)
        for c in range(2)
    ]
    return lax.ppermute(value, DP, perm)


def x_bits(x, c):
    high, mixed = x // 2, (x + x // 2) % 2
    return (mixed * (1 - c) + high * c, high * (1 - c) + mixed * c)


def pick(value, index, parts, dim):
    size = value.shape[dim] // parts
    return lax.dynamic_slice_in_dim(value, index * size, size, dim)


def send(value, partner, step):
    return trade(value.astype(LINK), partner, step).astype(jnp.float32)


def both(own, got, bit, dim):
    first = jnp.where(bit == 0, own, got)
    second = jnp.where(bit == 0, got, own)
    return jnp.concatenate([first, second], axis=dim)


def pick_z(value, index):
    mats, blocks, *rest = value.shape
    pairs = value.reshape(mats, blocks // 2, 2, *rest)
    return lax.dynamic_slice_in_dim(pairs, index, 1, 2).reshape(mats, blocks // 2, *rest)


def sum_x(value, bits, step):
    got = send(pick(value, 1 - bits[step], 2, 3), x_partner, step)
    return pick(value, bits[step], 2, 3) + got


def sum_z(value, odd):
    got = send(pick_z(value, 1 - odd), z_partner, 0)
    return pick_z(value, odd) + got


FAR = (1, 3, 2)
BACK = (2, 1, 3)


def sum_quad(value, place):
    got = [send(pick(value, (place + k) % 4, 4, 1), z_ahead, k) for k in FAR]
    return pick(value, place, 4, 1) + got[0] + got[1] + got[2]


def gather_quad(value, place):
    mats, _, *rest = value.shape
    got = [trade(value, z_ahead, k) for k in BACK]
    whole = jnp.zeros((mats, 4, *rest), value.dtype)
    for k, piece in zip((0, *BACK), (value, *got)):
        whole = lax.dynamic_update_slice_in_dim(whole, piece, (place - k) % 4, 1)
    return whole


def gather_x(value, bits, step):
    return both(value, trade(value, x_partner, step), bits[step], 3)


def gather_z(value, odd):
    mats, blocks, *rest = value.shape
    got = trade(value, z_partner, 0)
    own, got = (v.reshape(mats, blocks, 1, *rest) for v in (value, got))
    return both(own, got, odd, 2).reshape(mats, 2 * blocks, *rest)


def x_places(across, mine):
    masks = (1 + 2 * mine, 3 - 2 * mine)
    return (across, across ^ masks[0], across ^ masks[1], across ^ masks[0] ^ masks[1])


def split_step(groups, bits, step):
    give = jnp.concatenate([pick(v, 1 - bits[step], 2, 3) for v in groups], axis=2)
    got = trade(give, x_partner, step)
    groups = [pick(v, bits[step], 2, 3) for v in groups]
    return groups + [got[:, :, 4 * k : 4 * k + 4] for k in range(len(groups))]


def rows_in_order(groups, across, mine):
    one = groups[0]
    whole = jnp.zeros((*one.shape[:2], 16, one.shape[3]), one.dtype)
    for place, group in zip(x_places(across, mine), groups):
        whole = lax.dynamic_update_slice_in_dim(whole, group, 4 * place, 2)
    return whole


def join_columns(state, across, mine, bits):
    own, one, two, three = [pick(state, place, 4, 2) for place in x_places(across, mine)]
    got = trade(jnp.concatenate([one, three], axis=2), x_partner, 0)
    first = got[:, :, :4]
    got = trade(jnp.concatenate([two, got[:, :, 4:]], axis=2), x_partner, 1)
    place, width = 2 * bits[0] + bits[1], state.shape[3]
    left = jnp.zeros((*state.shape[:2], 4, 4 * width), state.dtype)
    for chunk, flip in zip((own, first, got[:, :, :4], got[:, :, 4:]), (0, 2, 1, 3)):
        left = lax.dynamic_update_slice_in_dim(left, chunk, width * (place ^ flip), 3)
    return left


def scale_kernel(at_ref, notes_ref, weight_ref, own_ref, raw_ref):
    totals = jnp.sum(notes_ref[...], axis=0).astype(jnp.float32)
    ratios = weight_ref[...] / totals
    lanes = lax.broadcasted_iota(jnp.int32, ratios.shape, 1)
    for j, out in enumerate((own_ref, raw_ref)):
        kind = notes_ref[at_ref[j]][:, 3:4]
        picked = jnp.sum(jnp.where(lanes == kind, ratios, 0.0), axis=1, keepdims=True)
        out[...] = jnp.broadcast_to(picked * RAISE, out.shape)


def scale_rows(notes, loss_weight, places, width):
    weight = jnp.pad(loss_weight, (0, 1))[None]
    return pl.pallas_call(
        scale_kernel,
        out_shape=[jax.ShapeDtypeStruct((1, width), jnp.float32)] * 2,
        in_specs=[
            pl.BlockSpec(memory_space=pltpu.SMEM),
            pl.BlockSpec(memory_space=pltpu.VMEM),
            pl.BlockSpec(memory_space=pltpu.VMEM),
        ],
        out_specs=[pl.BlockSpec(memory_space=pltpu.VMEM)] * 2,
        compiler_params=pltpu.CompilerParams(vmem_limit_bytes=1 << 20),
    )(places, notes, weight)


def tiles_kernel(at_ref, grad_ref, first_ref, second_ref, held, arrived, left):
    at = pl.multiple_of(at_ref[0], 128)
    outs = (first_ref, second_ref)
    mats, width = grad_ref.shape[0], first_ref.shape[3]
    places = [(t, m) for t in range(2) for m in range(mats)]
    ins = [
        pltpu.make_async_copy(grad_ref.at[m, :, t, :, pl.ds(at, width)], held.at[t, m], arrived.at[t, m])
        for t, m in places
    ]
    backs = [pltpu.make_async_copy(held.at[t, m], outs[t].at[m], left.at[t, m]) for t, m in places]
    for copy in ins:
        copy.start()
    for copy, back in zip(ins, backs):
        copy.wait()
        back.start()
    for back in backs:
        back.wait()


def tiles_of(grad, core, half):
    mats, blocks, _, rows, _ = grad.shape
    shape = (mats, blocks, rows, half)
    return pl.pallas_call(
        tiles_kernel,
        out_shape=[jax.ShapeDtypeStruct(shape, grad.dtype)] * 2,
        in_specs=[pl.BlockSpec(memory_space=pltpu.SMEM), pl.BlockSpec(memory_space=pl.ANY)],
        out_specs=[pl.BlockSpec(memory_space=pl.ANY)] * 2,
        scratch_shapes=[
            pltpu.VMEM((2, *shape), grad.dtype),
            pltpu.SemaphoreType.DMA((2, mats)),
            pltpu.SemaphoreType.DMA((2, mats)),
        ],
        cost_estimate=pl.CostEstimate(
            flops=0, bytes_accessed=4 * mats * blocks * rows * half * 4, transcendentals=0
        ),
    )((core * half)[None], grad)


def local(gradients, token_counts, modality, loss_weight, master, moment_one, moment_two):
    mats, rows, cols = 3, gradients.shape[1], gradients.shape[3]
    half = cols // 2
    depth, across, mine = (lax.axis_index(a) for a in DP)
    odd, place = depth % 2, depth // 2
    xb = x_bits(across, mine)

    notes = jnp.concatenate([token_counts, modality[:, None]], axis=1)
    notes = jnp.broadcast_to(notes, (DEEP * WIDE * 2, 4))[:, None]
    notes = lax.all_to_all(notes, DP, 0, 0, tiled=True)

    grad = jnp.transpose(gradients[0], (1, 0, 2)).reshape(mats, DEEP, 2, 8, cols)

    def tile(grad, t, core):
        cut = lax.dynamic_slice(grad, (0, 0, t, 0, core * half), (mats, DEEP, 1, 8, half))
        return cut.reshape(mats, DEEP, 8, half)

    give_a, give_b = tiles_of(grad, 1 - mine, half)
    raw_a = trade(give_a, core_partner)
    raw_b = trade(give_b, core_partner)
    raw = [raw_a, raw_b]

    state = jnp.stack([jnp.transpose(a, (1, 0, 2)) for a in (master, moment_one, moment_two)])
    got = trade(pick(state, 1 - mine, 2, 3), core_partner)
    state = both(pick(state, mine, 2, 3), got, mine, 2)

    chip = 2 * (WIDE * depth + across)
    scales = scale_rows(notes, loss_weight, jnp.stack([chip + mine, chip + 1 - mine]), half)

    def combined_a(index):
        own = pick_z(tile(grad, 0, mine), index)
        return own * scales[0] + pick_z(raw[0], index) * scales[1]

    def combined_b(index):
        at = mine * half + index * (half // 2)
        own = lax.dynamic_slice(grad, (0, 0, 1, 0, at), (mats, DEEP, 1, 8, half // 2))
        first, second = (scale[:, : half // 2] for scale in scales)
        return own[:, :, 0] * first + pick(raw[1], index, 2, 3) * second

    give_a = combined_a(1 - odd).astype(LINK)
    give_b = combined_b(1 - xb[0]).astype(LINK)
    raw_a, give_a = lax.optimization_barrier((raw[0], give_a))
    raw_b, give_b = lax.optimization_barrier((raw[1], give_b))
    raw = [raw_a, raw_b]
    part_a = lax.optimization_barrier(combined_a(odd))
    part_b = lax.optimization_barrier(combined_b(xb[0]))
    got_a = send(give_a, z_partner, 0)
    got_b = send(give_b, x_partner, 0)
    part_a, part_b = part_a + got_a, part_b + got_b
    part_a = sum_x(part_a, xb, 0)
    part_b = sum_z(part_b, odd)
    groups = split_step([state], xb, 0)
    part = jnp.concatenate([part_a, part_b], axis=2)
    give_c = pick(part, 1 - xb[1], 2, 3).astype(LINK)
    got = trade(give_c, x_partner, 1)
    groups = split_step(groups, xb, 1)
    part = lax.optimization_barrier(pick(part, xb[1], 2, 3) + got.astype(jnp.float32))

    state = rows_in_order(groups, across, mine)

    summed = sum_quad(part, place)[:, 0] * (1.0 / RAISE)
    weights_new, _, _ = adam_update(summed, state[1], state[2], state[0])
    lean = weights_new.astype(jnp.bfloat16)[:, None]

    lean = gather_quad(lean, place)
    lean = gather_x(lean, xb, 1)
    lean_b = gather_z(lean[:, :, 8:], odd)
    lean_a = gather_x(lean[:, :, :8], xb, 0)
    got_a, got_b = trade(lean_a, z_partner), trade(lean_b, x_partner, 0)
    whole = jnp.zeros((mats, DEEP // 2, 2, 2, 8, cols), jnp.bfloat16)
    for core in (mine, 1 - mine):
        side = x_bits(across, core)[0]
        for tile_a, tile_b, place_a, place_b in (
            (lean_a, lean_b, odd, side),
            (got_a, got_b, 1 - odd, 1 - side),
        ):
            if core is not mine:
                tile_a, tile_b = trade(tile_a, core_partner), trade(tile_b, core_partner)
            tile_a = tile_a[:, :, None, None]
            whole = lax.dynamic_update_slice(whole, tile_a, (0, 0, place_a, 0, 0, core * half))
            tile_b = tile_b.reshape(mats, DEEP // 2, 2, 1, 8, half // 2)
            at = core * half + place_b * (half // 2)
            whole = lax.dynamic_update_slice(whole, tile_b, (0, 0, 0, 1, 0, at))
    whole = whole.reshape(mats, rows, cols)

    left = join_columns(summed[None], across, mine, xb)
    back = both(pick(left, mine, 2, 2), trade(pick(left, 1 - mine, 2, 2), core_partner), mine, 3)[0]
    turned = [jnp.transpose(a, (1, 0, 2)) for a in (moment_one, moment_two, master)]
    outs = [jnp.transpose(a, (1, 0, 2)) for a in adam_update(back, *turned)]
    return (*outs, jnp.transpose(whole, (1, 0, 2)))


def solution(mesh):
    torus = Mesh(mesh.devices.reshape(DEEP, WIDE, 2, mesh.shape["tensor"]), (*DP, "tensor"))
    in_specs = (
        P(DP, None, None, "tensor"),
        P(DP, None),
        P(DP),
        P(),
        P(DP, None, "tensor"),
        P(DP, None, "tensor"),
        P(DP, None, "tensor"),
    )
    out_specs = (
        P(DP, None, "tensor"),
        P(DP, None, "tensor"),
        P(DP, None, "tensor"),
        P(None, None, "tensor"),
    )

    return jax.shard_map(local, mesh=torus, in_specs=in_specs, out_specs=out_specs, check_vma=False)
```
